32 devices in a mesh: slot: 4 (over x, core), query: 8 (over z, y).
Axes of the slice: x: 2, y: 2, z: 4, core: 2. Of those that a mesh axis runs over, the one named last changes fastest.
Arguments:
- hidden_in: bfloat16 [2, 8, 4, 128, 768], P(None, 'query', 'slot'), may hold values from -6 to 6
- token_mask: int32 [2, 8, 4, 128], P(None, 'query', 'slot'), may hold values from 0 to 1, as said below
- masked_pos: int32 [2, 8, 4, 20], P(None, 'query', 'slot'), may hold values from 1 to 127, as said below
- targets: int32 [2, 8, 4, 20], P(None, None, 'slot'), may hold values from 0 to 30719
- slot_mask: int32 [2, 8, 4], P(None, 'query', 'slot'), may hold values from 0 to 1, as said below
- query_embed: bfloat16 [2, 8, 128], P(None, 'query', 'slot'), may hold values from -0.8984375 to 0.8984375
- w_qkv: bfloat16 [768, 2304], replicated, may hold values from -0.3125 to 0.3125
- b_query: bfloat16 [768], replicated, may hold values from -1.75 to 1.75
- b_value: bfloat16 [768], replicated, may hold values from -1.75 to 1.75
- w_out: bfloat16 [768, 768], replicated, may hold values from -1.25 to 1.25
- b_out: bfloat16 [768], replicated, may hold values from -1.75 to 1.75
- gain_first: bfloat16 [768], replicated, may hold values from 0.25 to 1.75
- shift_first: bfloat16 [768], replicated, may hold values from -1.25 to 1.25
- w_in: bfloat16 [768, 3072], replicated, may hold values from -0.21875 to 0.21875
- b_in: bfloat16 [3072], replicated, may hold values from -1.75 to 1.75
- w_ffn_out: bfloat16 [3072, 768], replicated, may hold values from -0.109375 to 0.109375
- b_ffn_out: bfloat16 [768], replicated, may hold values from -1.75 to 1.75
- gain_second: bfloat16 [768], replicated, may hold values from 0.25 to 1.75
- shift_second: bfloat16 [768], replicated, may hold values from -1.25 to 1.25
- w_retr: bfloat16 [768, 128], replicated, may hold values from -0.21875 to 0.21875
- word_table: bfloat16 [30720, 768], P('query'), may hold values from -0.65625 to 0.65625
Outputs:
- marginal: float32 [2, 8], P(None, 'query')
- layer_out: bfloat16 [2, 8, 4, 128, 768], P(None, 'query', 'slot')
- hidden_grad: float32 [2, 8, 4, 128, 768], P(None, 'query', 'slot')
- query_grad: float32 [2, 8, 128], P(None, 'query', 'slot')
- w_qkv_grad: float32 [768, 2304], P('query')
- b_query_grad: float32 [768], P('query')
- b_value_grad: float32 [768], P('query')
- w_out_grad: float32 [768, 768], P('query')
- b_out_grad: float32 [768], P('query')
- gain_first_grad: float32 [768], P('query')
- shift_first_grad: float32 [768], P('query')
- w_in_grad: float32 [768, 3072], P('query')
- b_in_grad: float32 [3072], P('query')
- w_ffn_out_grad: float32 [3072, 768], P('query')
- b_ffn_out_grad: float32 [768], P('query')
- gain_second_grad: float32 [768], P('query')
- shift_second_grad: float32 [768], P('query')
- w_retr_grad: float32 [768, 128], P('query')
- word_table_grad: float32 [30720, 768], P('query')
The draws below stay inside these ranges and needn't reach their ends.
Inputs may be any that keep to these rules, and one draw needn't show every extreme that they name: `token_mask`: each sequence's mask is 1 on its first 64 to 128 tokens and 0 after them. `masked_pos`: each position lies after the first token and among its sequence's tokens with mask 1; positions within a sequence may repeat. `slot_mask`: each query has 2 to 4 slots with mask 1, in any places.
All inputs are finite; a program needn't handle non-finite values.
Results may differ from the reference program's by a relative error of at most 0.025.
Values may be sent and summed in bfloat16 or wider, within the bound.
No kernel may reach another device: no remote copies, remote signals or barrier semaphores. Data moves between devices by JAX's collectives and lax.ppermute only.
A program may use at most 256 MiB of HBM per device.

```python
import jax
import jax.numpy as jnp
from jax import lax

D = 768
HEAD = 64
FF = 3072
RD = 128
VOCAB = 30720
SEQ = 128
MASKED = 20
MICRO = 2
QUERIES = 8
SLOTS = 4


def token_layout(key):
    key = jax.random.fold_in(key, 11)
    length_key, place_key = jax.random.split(key)
    lengths = jax.random.randint(length_key, (MICRO, QUERIES, SLOTS, 1), SEQ // 2, SEQ + 1)
    places = jax.random.randint(place_key, (MICRO, QUERIES, SLOTS, MASKED), 1, lengths)
    return (lengths, places)


def draw_token_mask(key, part):
    lengths, places = token_layout(key)
    columns = jnp.arange(SEQ, dtype=jnp.int32)[None, None, None, :]
    return (columns < lengths).astype(jnp.int32)


def draw_masked_pos(key, part):
    lengths, places = token_layout(key)
    return places.astype(jnp.int32)


def draw_slot_mask(key, part):
    key = jax.random.fold_in(key, 7)
    count_key, order_key = jax.random.split(key)
    counts = jax.random.randint(count_key, (MICRO, QUERIES, 1), SLOTS // 2, SLOTS + 1)
    orders = jax.random.randint(order_key, (MICRO, QUERIES, SLOTS), 0, 1 << 20) * SLOTS + jnp.arange(SLOTS, dtype=jnp.int32)
    ranks = jnp.argsort(jnp.argsort(orders, axis=-1), axis=-1)
    return (ranks < counts).astype(jnp.int32)


def place_ends(values, rng, low, high):
    longest = values.shape.index(max(values.shape))
    spots = []
    for shift in (0, 1):
        where = [jax.random.randint(jax.random.fold_in(rng, axis), (), 0, length) for axis, length in enumerate(values.shape)]
        where[longest] = (where[longest] + shift) % values.shape[longest]
        spots.append(tuple(where))
    return values.at[spots[0]].set(low).at[spots[1]].set(high)


def level_of(rng, extent, shards, least, largest):
    def one(dim, shards_of):
        heights = jax.random.uniform(jax.random.fold_in(jax.random.fold_in(rng, 6), dim), (shards_of,), jnp.float32, least / len(shards), largest / len(shards))
        return jnp.repeat(jnp.exp(heights), extent[dim] // shards_of).reshape((-1,) + (1,) * (len(extent) - dim - 1))

    level = one(*shards[0])
    for cut in shards[1:]:
        level = level * one(*cut)
    return level


def gaussian(own_key, extent, scale, reach, cuts=(), kind=jnp.bfloat16):
    factor_of = level_of(own_key, extent, cuts, -0.22, 0.18) if cuts else 1.0
    array = jax.random.normal(own_key, extent, jnp.float32) * scale * factor_of
    return jnp.minimum(jnp.maximum(array, -reach), reach).astype(kind)


def setup_inputs(seed: int = 0) -> dict:
    splits = jax.random.split(jax.random.key(seed), 22)
    return {
        "hidden_in": gaussian(splits[0], (MICRO, QUERIES, SLOTS, SEQ, D), 1.0, 6.0, ((1, 8), (2, 4))),
        "token_mask": draw_token_mask(jax.random.fold_in(splits[21], 71), 0),
        "masked_pos": draw_masked_pos(jax.random.fold_in(splits[21], 71), 0),
        "targets": place_ends(jax.random.randint(splits[3], (MICRO, QUERIES, SLOTS, MASKED), 0, VOCAB), jax.random.fold_in(splits[3], 1), 0, VOCAB - 1).astype(jnp.int32),
        "slot_mask": draw_slot_mask(jax.random.fold_in(splits[21], 71), 0),
        "query_embed": gaussian(splits[5], (MICRO, QUERIES, RD), 0.15, 0.8984375, ((1, 8), (2, 4))),
        "w_qkv": gaussian(splits[6], (D, 3 * D), (D // 2) ** -0.5, 0.3125),
        "b_query": gaussian(splits[7], (D,), 0.3, 1.75),
        "b_value": gaussian(splits[8], (D,), 0.3, 1.75),
        "w_out": gaussian(splits[9], (D, D), (D // 32) ** -0.5, 1.25),
        "b_out": gaussian(splits[10], (D,), 0.3, 1.75),
        "gain_first": jnp.clip(1.0 + 0.15 * jax.random.normal(splits[11], (D,), jnp.float32), 0.25, 1.75).astype(jnp.bfloat16),
        "shift_first": gaussian(splits[12], (D,), 0.2, 1.25),
        "w_in": gaussian(splits[13], (D, FF), D ** -0.5, 0.21875),
        "b_in": gaussian(splits[14], (FF,), 0.3, 1.75),
        "w_ffn_out": gaussian(splits[15], (FF, D), FF ** -0.5, 0.109375),
        "b_ffn_out": gaussian(splits[16], (D,), 0.3, 1.75),
        "gain_second": jnp.clip(1.0 + 0.15 * jax.random.normal(splits[17], (D,), jnp.float32), 0.25, 1.75).astype(jnp.bfloat16),
        "shift_second": gaussian(splits[18], (D,), 0.2, 1.25),
        "w_retr": gaussian(splits[19], (D, RD), D ** -0.5, 0.21875),
        "word_table": gaussian(splits[20], (VOCAB, D), 0.11, 0.65625, ((0, 8),)),
    }


@jax.custom_vjp
def low(v):
    return lax.optimization_barrier(v.astype(jnp.bfloat16)).astype(jnp.float32)

@jax.custom_vjp
def low_back(v):
    return v

def low_keep(v):
    return (low(v), None)

def low_pass(kept, grad):
    return (grad,)

def back_keep(v):
    return (v, None)

def back_low(kept, grad):
    return (low(grad),)
low.defvjp(low_keep, low_pass)
low_back.defvjp(back_keep, back_low)
NEG_FILL = -1e+30
NORM_EPS = 1e-12
TOP_PRECISION = lax.Precision.HIGHEST

def layer_norm(summed, gain_vec, shift_vec):
    centre = summed - lax.optimization_barrier(jnp.mean(summed, axis=-1, keepdims=True))
    variance = lax.optimization_barrier(jnp.mean(centre * centre, axis=-1, keepdims=True))
    return centre * lax.rsqrt(variance + NORM_EPS) * gain_vec + shift_vec

def micro_forward(micro_batch, params):
    hidden, token_mask, masked_pos, targets, slot_mask, query_embed = micro_batch
    w_qkv, b_query, b_value, w_out, b_out, gain_first, shift_first, w_in, b_in, w_ffn_out, b_ffn_out, gain_second, shift_second, w_retr, word_table = params
    query_count, slot_count, seq_len, width = hidden.shape
    seq_count = query_count * slot_count
    head_count = width // HEAD
    hidden = hidden.reshape(seq_count, seq_len, width)
    key_ok = token_mask.reshape(seq_count, seq_len) > 0
    qkv_bias = jnp.concatenate([b_query, jnp.zeros_like(b_query), b_value])
    united_qkv = jnp.einsum('bld,de->ble', hidden, w_qkv, precision=TOP_PRECISION) + qkv_bias
    united_qkv = low(low_back(united_qkv))
    head_shape = (seq_count, seq_len, head_count, HEAD)
    query_part = united_qkv[..., :width].reshape(head_shape)
    key_part = united_qkv[..., width:2 * width].reshape(head_shape)
    value_part = united_qkv[..., 2 * width:].reshape(head_shape)
    score_scale = HEAD ** (-0.5)
    scores = low_back(jnp.einsum('bqhd,bkhd->bhqk', query_part, key_part, precision=TOP_PRECISION) * score_scale)
    scores = jnp.where(key_ok[:, None, None, :], scores, NEG_FILL)
    attn_probs = jax.nn.softmax(scores, axis=-1)
    context = jnp.einsum('bhqk,bkhd->bqhd', low(attn_probs), value_part, precision=TOP_PRECISION)
    context = low(low_back(context.reshape(seq_count, seq_len, width)))
    attended = low_back(jnp.einsum('bld,de->ble', context, w_out, precision=TOP_PRECISION) + b_out)
    first_out = layer_norm(hidden + attended, gain_first, shift_first)
    inner_pre = low_back(jnp.einsum('bld,df->blf', low(first_out), w_in, precision=TOP_PRECISION) + b_in)
    active = low(jax.nn.gelu(inner_pre, approximate=False))
    branch = low_back(jnp.einsum('blf,fd->bld', active, w_ffn_out, precision=TOP_PRECISION) + b_ffn_out)
    second = layer_norm(branch + first_out, gain_second, shift_second)
    cls_rows = low(second[:, 0, :])
    document = jnp.dot(cls_rows, w_retr, precision=TOP_PRECISION).reshape(query_count, slot_count, -1)
    retr_score = jnp.einsum('qsr,qr->qs', document, query_embed, precision=TOP_PRECISION)
    positions = masked_pos.reshape(seq_count, -1).astype(jnp.int32)
    picked = low(jnp.take_along_axis(second, positions[:, :, None], axis=1))
    logits = low_back(jnp.einsum('bmd,vd->bmv', picked, word_table, precision=TOP_PRECISION))
    normal = jax.nn.logsumexp(logits, axis=-1)
    target_ids = targets.reshape(seq_count, -1).astype(jnp.int32)
    chosen = jnp.take_along_axis(logits, target_ids[:, :, None], axis=2)[..., 0]
    likely = lax.optimization_barrier(jnp.mean(chosen - normal, axis=-1)).reshape(query_count, slot_count)
    slot_valid = slot_mask > 0
    joint_lse = jax.nn.logsumexp(jnp.where(slot_valid, retr_score + likely, NEG_FILL), axis=-1)
    prior_lse = jax.nn.logsumexp(jnp.where(slot_valid, retr_score, NEG_FILL), axis=-1)
    return (joint_lse - prior_lse, second.reshape(query_count, slot_count, seq_len, width))

def reference(hidden_in, token_mask, masked_pos, targets, slot_mask, query_embed, w_qkv, b_query, b_value, w_out, b_out, gain_first, shift_first, w_in, b_in, w_ffn_out, b_ffn_out, gain_second, shift_second, w_retr, word_table):
    floats = [value.astype(jnp.float32) for value in (hidden_in, query_embed, w_qkv, b_query, b_value, w_out, b_out, gain_first, shift_first, w_in, b_in, w_ffn_out, b_ffn_out, gain_second, shift_second, w_retr, word_table)]

    def objective(hidden, queries, *params):
        margin_parts = []
        layer_parts = []
        for micro_step in range(MICRO):
            micro_batch = (hidden[micro_step], token_mask[micro_step], masked_pos[micro_step], targets[micro_step], slot_mask[micro_step], queries[micro_step])
            margin_one, layer_one = micro_forward(micro_batch, params)
            margin_parts.append(margin_one)
            layer_parts.append(layer_one)
        margins = jnp.stack(margin_parts)
        layer_all = jnp.stack(layer_parts)
        return (-jnp.sum(margins), (margins, layer_all))
    objective_value, pullback, (margins, layer_all) = jax.vjp(objective, *floats, has_aux=True)
    gradients = pullback(jnp.ones_like(objective_value))
    return (margins, layer_all.astype(jnp.bfloat16), gradients[0], gradients[1], gradients[2], gradients[3], gradients[4], gradients[5], gradients[6], gradients[7], gradients[8], gradients[9], gradients[10], gradients[11], gradients[12], gradients[13], gradients[14], gradients[15], gradients[16])
```

```python
import functools

import jax
import jax.numpy as jnp
from jax import lax
from jax.sharding import PartitionSpec as P

HEAD = 64
NEG_FILL = -1e30
NORM_EPS = 1e-12
TOP_PRECISION = lax.Precision.HIGHEST
ROOT_HALF = 0.7071067811865476
DENSITY_SCALE = 0.3989422804014327
BF = jnp.bfloat16
F32 = jnp.float32


def times_right(left_side, right_side):
    return lax.dot_general(
        left_side,
        right_side,
        (((left_side.ndim - 1,), (0,)), ((), ())),
        preferred_element_type=F32,
    )


def times_transposed(left_side, right_side):
    return lax.dot_general(
        left_side,
        right_side,
        (((left_side.ndim - 1,), (1,)), ((), ())),
        preferred_element_type=F32,
    )


def token_outer(left_side, right_side):
    return lax.dot_general(
        left_side, right_side, (((0,), (0,)), ((), ())), preferred_element_type=F32
    )


def norm_forward(summed, gain_vec, shift_vec):
    centre = summed - jnp.mean(summed, axis=-1, keepdims=True)
    inverse = lax.rsqrt(jnp.mean(centre * centre, axis=-1, keepdims=True) + NORM_EPS)
    normed = centre * inverse
    return (normed * gain_vec + shift_vec, normed, inverse)


def norm_backward(grad_out, normed, inverse, gain_vec):
    grad_normed = grad_out * gain_vec
    mean_grad = jnp.mean(grad_normed, axis=-1, keepdims=True)
    mean_proj = jnp.mean(grad_normed * normed, axis=-1, keepdims=True)
    grad_input = inverse * (grad_normed - mean_grad - normed * mean_proj)
    return (grad_input, jnp.sum(grad_out * normed, axis=0), jnp.sum(grad_out, axis=0))


def gelu_value(inner_pre):
    return 0.5 * inner_pre * (1.0 + lax.erf(inner_pre * ROOT_HALF))


def gelu_slope(inner_pre):
    return (
        0.5 * (1.0 + lax.erf(inner_pre * ROOT_HALF))
        + inner_pre * jnp.exp(-0.5 * inner_pre * inner_pre) * DENSITY_SCALE
    )


def swap(value, axis, count, bit):
    pairs = [(i, i ^ (1 << bit)) for i in range(count)]
    return lax.ppermute(value, axis, pairs)


def pick(value, index, dim):
    return lax.dynamic_index_in_dim(value, index, dim, keepdims=False)


def per_device(
    n_q,
    n_s,
    hidden_in,
    token_mask,
    masked_pos,
    targets,
    slot_mask,
    query_embed,
    w_qkv,
    b_query,
    b_value,
    w_out,
    b_out,
    gain_first,
    shift_first,
    w_in,
    b_in,
    w_ffn_out,
    b_ffn_out,
    gain_second,
    shift_second,
    w_retr,
    word_table,
):
    micro, _, _, seq_len, width = hidden_in.shape
    masked = masked_pos.shape[-1]
    tokens = micro * seq_len
    heads = width // HEAD
    inner = w_in.shape[1]
    vocab_own = word_table.shape[0]
    own_rows = micro * masked
    score_scale = HEAD ** (-0.5)
    q_bits = n_q.bit_length() - 1
    s_bits = n_s.bit_length() - 1
    q_me = lax.axis_index("query")
    s_me = lax.axis_index("slot")

    q_order = q_me ^ jnp.arange(n_q, dtype=jnp.int32)

    def gather_query(value):
        out = value[None]
        for bit in reversed(range(q_bits)):
            out = jnp.concatenate([out, swap(out, "query", n_q, bit)], axis=0)
        return out

    rel = []
    for block in range(n_q):
        offset = 0
        for step, bit in enumerate(reversed(range(q_bits))):
            if block >> step & 1:
                offset |= 1 << bit
        rel.append(offset)
    q_order = q_me ^ jnp.array(rel, jnp.int32)

    query_full = lax.all_gather(query_embed, "slot", axis=2, tiled=True)[:, 0].astype(F32)

    own_targets = jnp.take(targets[:, :, 0, :].transpose(1, 0, 2), q_order, axis=0).reshape(-1)
    local_targets = own_targets - q_me * vocab_own
    target_hit = local_targets[:, None] == lax.iota(jnp.int32, vocab_own)[None, :]
    rows = times_right(target_hit.astype(BF), word_table).astype(BF).reshape(n_q, own_rows, width)
    for bit in range(q_bits):
        half = rows.shape[0] // 2
        rows = rows[:half] + swap(rows[half:], "query", n_q, bit)
    target_rows = rows[0].astype(F32)

    hidden = hidden_in.reshape(tokens, width)
    key_ok = token_mask.reshape(micro, seq_len) > 0
    qkv_bias = jnp.concatenate([b_query, jnp.zeros_like(b_query), b_value]).astype(F32)
    gain_one = gain_first.astype(F32)
    gain_two = gain_second.astype(F32)
    united = (times_right(hidden, w_qkv) + qkv_bias).astype(BF)
    head_shape = (micro, seq_len, heads, HEAD)
    query_part = united[:, :width].reshape(head_shape)
    key_part = united[:, width : 2 * width].reshape(head_shape)
    value_part = united[:, 2 * width :].reshape(head_shape)
    scores = (
        jnp.einsum("bqhd,bkhd->bhqk", query_part, key_part, preferred_element_type=F32)
        * score_scale
    )
    scores = jnp.where(key_ok[:, None, None, :], scores, NEG_FILL)
    probs = jax.nn.softmax(scores, axis=-1)
    probs_low = probs.astype(BF)
    context = jnp.einsum("bhqk,bkhd->bqhd", probs_low, value_part, preferred_element_type=F32)
    context = context.reshape(tokens, width).astype(BF)
    attended = times_right(context, w_out) + b_out.astype(F32)
    first_out, first_normed, first_inverse = norm_forward(
        hidden.astype(F32) + attended, gain_one, shift_first.astype(F32)
    )
    first_low = first_out.astype(BF)
    inner_pre = times_right(first_low, w_in) + b_in.astype(F32)
    active = gelu_value(inner_pre).astype(BF)
    branch = times_right(active, w_ffn_out) + b_ffn_out.astype(F32)
    second, second_normed, second_inverse = norm_forward(
        branch + first_out, gain_two, shift_second.astype(F32)
    )
    second_low = second.astype(BF).reshape(micro, seq_len, width)
    layer_out = second_low.reshape(hidden_in.shape)

    positions = masked_pos.reshape(micro, masked)
    place = (positions[:, :, None] == lax.iota(jnp.int32, seq_len)[None, None, :]).astype(BF)
    picked = (
        jnp.einsum("bml,bld->bmd", place, second_low, preferred_element_type=F32)
        .astype(BF)
        .reshape(own_rows, width)
    )
    cls_rows = second_low[:, 0, :]
    document = times_right(cls_rows, w_retr)
    retr_score = jnp.sum(document * query_full, axis=-1)
    picked_q = gather_query(picked).reshape(n_q * own_rows, width)

    logits = times_transposed(picked_q, word_table)
    top = jnp.max(logits, axis=-1, keepdims=True)
    powers = jnp.exp(logits - top)
    total = jnp.sum(powers, axis=-1, keepdims=True)
    chosen = jnp.sum(jnp.where(target_hit, logits, 0.0), axis=-1, keepdims=True)
    others = jnp.where(target_hit, 0.0, powers).astype(BF)
    pulled = times_right(others, word_table).reshape(n_q, own_rows, width)
    stats = jnp.stack([top, total, chosen], axis=0).reshape(3, n_q, own_rows)
    for bit in range(q_bits):
        half = pulled.shape[0] // 2
        pulled_in = swap(pulled[half:].astype(BF), "query", n_q, bit).astype(F32)
        stats_in = swap(stats[:, half:], "query", n_q, bit)
        pulled, stats = pulled[:half], stats[:, :half]
        new_top = jnp.maximum(stats[0], stats_in[0])
        keep_scale = jnp.exp(stats[0] - new_top)
        in_scale = jnp.exp(stats_in[0] - new_top)
        pulled = pulled * keep_scale[..., None] + pulled_in * in_scale[..., None]
        stats = jnp.stack(
            [
                new_top,
                stats[1] * keep_scale + stats_in[1] * in_scale,
                stats[2] + stats_in[2],
            ],
            axis=0,
        )
    row_top, row_total, row_chosen = stats[0, 0], stats[1, 0], stats[2, 0]
    normal = row_top + jnp.log(row_total)
    row_ll = row_chosen - normal
    likely = jnp.mean(row_ll.reshape(micro, masked), axis=-1)

    valid = slot_mask.reshape(micro).astype(F32)
    packed = jnp.concatenate(
        [document, retr_score[:, None], likely[:, None], valid[:, None]], axis=-1
    )
    slots = lax.all_gather(packed, "slot", axis=0)
    documents = slots[:, :, :-3]
    slot_ok = slots[:, :, -1] > 0
    slot_score = jnp.where(slot_ok, slots[:, :, -3], NEG_FILL)
    slot_joint = jnp.where(slot_ok, slots[:, :, -3] + slots[:, :, -2], NEG_FILL)
    prior_lse = jax.nn.logsumexp(slot_score, axis=0)
    joint_lse = jax.nn.logsumexp(slot_joint, axis=0)
    marginal = (joint_lse - prior_lse)[:, None]
    prior = jnp.where(slot_ok, jnp.exp(slot_score - prior_lse), 0.0)
    post = jnp.where(slot_ok, jnp.exp(slot_joint - joint_lse), 0.0)
    grad_scores_all = prior - post
    part = query_embed.shape[2]
    doc_part = lax.dynamic_slice_in_dim(documents, s_me * part, part, 2)
    query_grad = jnp.sum(grad_scores_all[:, :, None] * doc_part, axis=0)[:, None, :]
    own_post = pick(post, s_me, 0)
    own_grad_score = pick(grad_scores_all, s_me, 0)
    grad_document = own_grad_score[:, None] * query_full
    w_retr_grad = jnp.dot(cls_rows.astype(F32).T, grad_document, precision=TOP_PRECISION)
    grad_cls = jnp.dot(grad_document, w_retr.astype(F32).T, precision=TOP_PRECISION)

    weight = jnp.broadcast_to((own_post / masked)[:, None], (micro, masked)).reshape(own_rows)
    hit_part = jnp.exp(row_ll) - 1.0
    grad_picked = weight[:, None] * (
        pulled[0] * (1.0 / row_total)[:, None] + hit_part[:, None] * target_rows
    )
    spread = jnp.concatenate(
        [place.astype(F32), (lax.iota(jnp.int32, seq_len) == 0).astype(F32)[None, None, :] * jnp.ones((micro, 1, 1), F32)],
        axis=1,
    )
    grad_rows = jnp.concatenate([grad_picked.reshape(micro, masked, width), grad_cls[:, None]], axis=1)
    grad_second = jnp.einsum(
        "bml,bmd->bld", spread, grad_rows, precision=TOP_PRECISION
    ).reshape(tokens, width)

    grad_sum_two, gain_two_grad, shift_two_grad = norm_backward(
        grad_second, second_normed, second_inverse, gain_two
    )
    grad_branch = grad_sum_two.astype(BF)
    grad_inner = (times_transposed(grad_branch, w_ffn_out) * gelu_slope(inner_pre)).astype(BF)
    grad_first = times_transposed(grad_inner, w_in) + grad_sum_two
    grad_sum_one, gain_one_grad, shift_one_grad = norm_backward(
        grad_first, first_normed, first_inverse, gain_one
    )
    grad_attended = grad_sum_one.astype(BF)
    grad_context = times_transposed(grad_attended, w_out).astype(BF).reshape(head_shape)
    grad_probs = jnp.einsum(
        "bqhd,bkhd->bhqk", grad_context, value_part, preferred_element_type=F32
    )
    grad_value = jnp.einsum("bhqk,bqhd->bkhd", probs_low, grad_context, preferred_element_type=F32)
    row_delta = jnp.sum(probs * grad_probs, axis=-1, keepdims=True)
    grad_scores = (probs * (grad_probs - row_delta)).astype(BF)
    grad_query = (
        jnp.einsum("bhqk,bkhd->bqhd", grad_scores, key_part, preferred_element_type=F32)
        * score_scale
    )
    grad_key = (
        jnp.einsum("bhqk,bqhd->bkhd", grad_scores, query_part, preferred_element_type=F32)
        * score_scale
    )
    grad_united = jnp.concatenate(
        [
            grad_query.reshape(tokens, width),
            grad_key.reshape(tokens, width),
            grad_value.reshape(tokens, width),
        ],
        axis=-1,
    ).astype(BF)
    hidden_grad = (times_transposed(grad_united, w_qkv) + grad_sum_one).reshape(hidden_in.shape)

    def column_sum(value):
        return jnp.sum(value.astype(F32), axis=0)

    united_sum = column_sum(grad_united)
    vectors = [
        united_sum[:width],
        united_sum[2 * width :],
        column_sum(grad_attended),
        gain_one_grad,
        shift_one_grad,
        column_sum(grad_inner),
        column_sum(grad_branch),
        gain_two_grad,
        shift_two_grad,
    ]

    def scatter_sum(value, order):
        total_rows, columns = value.shape
        rows_q = total_rows // n_q
        shape = [2] * q_bits + [2] * (s_bits - 1) + [rows_q >> (s_bits - 1), 2, columns // 2]
        addends = [value.reshape(shape)]
        labels = (
            [("query", b) for b in reversed(range(q_bits))]
            + [("slot", b) for b in reversed(range(1, s_bits))]
            + [None, ("slot", 0)]
        )
        for axis, bit in order:
            dim = labels.index((axis, bit))
            labels.pop(dim)
            me, count = (q_me, n_q) if axis == "query" else (s_me, n_s)
            mine = (me >> bit) & 1
            out = functools.reduce(
                jnp.add, [pick(a, 1 - mine, dim).astype(F32) for a in addends]
            ).astype(BF)
            addends = [pick(a, mine, dim) for a in addends] + [swap(out, axis, count, bit)]
        own = functools.reduce(jnp.add, [a.astype(F32) for a in addends]).astype(BF)
        for bit in range(1, s_bits):
            other = swap(own, "slot", n_s, bit)
            mine = (s_me >> bit) & 1
            low = jnp.where(mine == 0, own, other)
            high = jnp.where(mine == 0, other, own)
            own = jnp.concatenate([low, high], axis=0)
        other = swap(own, "slot", n_s, 0)
        mine = s_me & 1
        low = jnp.where(mine == 0, own, other)
        high = jnp.where(mine == 0, other, own)
        return jnp.concatenate([low, high], axis=1).astype(F32)

    core = [("slot", 0)]
    x_steps = [("slot", b) for b in range(1, s_bits)]
    y_steps = [("query", 0)]
    z_steps = [("query", b) for b in range(1, q_bits)]
    order_a = core + x_steps + y_steps + z_steps
    order_b = core + y_steps + x_steps + z_steps

    w_ffn_out_grad = scatter_sum(token_outer(active, grad_branch).astype(BF), order_a)
    w_in_grad = scatter_sum(token_outer(first_low, grad_inner).astype(BF), order_b)
    w_out_grad = scatter_sum(token_outer(context, grad_attended).astype(BF), order_a)
    w_qkv_grad = scatter_sum(token_outer(hidden, grad_united).astype(BF), order_b)

    small = jnp.concatenate(
        [w_retr_grad.reshape(n_q, -1)] + [v.reshape(n_q, -1) for v in vectors], axis=1
    )
    used = small.shape[1]
    lanes = 128 * 2 * (n_s // 2) * 8
    padded = -(-used // lanes) * lanes
    small = jnp.pad(small, ((0, 0), (0, padded - used))).astype(BF)
    small = small.reshape(n_q * (padded // 256), 256)
    small = scatter_sum(small, order_a).reshape(-1)
    retr_size = w_retr_grad.size // n_q
    w_retr_out = small[:retr_size].reshape(-1, w_retr.shape[1])
    vector_out = []
    start = retr_size
    for v in vectors:
        vector_out.append(small[start : start + v.size // n_q])
        start += v.size // n_q
    (
        b_query_grad,
        b_value_grad,
        b_out_grad,
        gain_one_out,
        shift_one_out,
        b_in_grad,
        b_ffn_grad,
        gain_two_out,
        shift_two_out,
    ) = vector_out

    picked_all = lax.all_gather(picked_q, "slot", axis=0, tiled=True)
    row_info = jnp.stack([normal, weight], axis=0)
    info_q = gather_query(row_info).transpose(1, 0, 2).reshape(2, n_q * own_rows)
    info_all = lax.all_gather(info_q, "slot", axis=0)
    targets_all = lax.all_gather(own_targets, "slot", axis=0, tiled=True) - q_me * vocab_own
    normal_all = info_all[:, 0].reshape(-1, 1)
    weight_all = info_all[:, 1].reshape(-1, 1)
    logits_all = times_transposed(picked_all, word_table)
    hit_all = targets_all[:, None] == lax.iota(jnp.int32, vocab_own)[None, :]
    grad_logits = (
        weight_all * (jnp.exp(logits_all - normal_all) - hit_all.astype(F32))
    ).astype(BF)
    table_grad = token_outer(grad_logits, picked_all)

    return (
        marginal,
        layer_out,
        hidden_grad,
        query_grad,
        w_qkv_grad,
        b_query_grad,
        b_value_grad,
        w_out_grad,
        b_out_grad,
        gain_one_out,
        shift_one_out,
        w_in_grad,
        b_in_grad,
        w_ffn_out_grad,
        b_ffn_grad,
        gain_two_out,
        shift_two_out,
        w_retr_out,
        table_grad,
    )


def solution(mesh):
    return jax.shard_map(
        functools.partial(per_device, mesh.shape["query"], mesh.shape["slot"]),
        mesh=mesh,
        in_specs=(
            P(None, "query", "slot", None, None),
            P(None, "query", "slot", None),
            P(None, "query", "slot", None),
            P(None, None, "slot", None),
            P(None, "query", "slot"),
            P(None, "query", "slot"),
            P(),
            P(),
            P(),
            P(),
            P(),
            P(),
            P(),
            P(),
            P(),
            P(),
            P(),
            P(),
            P(),
            P(),
            P("query", None),
        ),
        out_specs=(
            P(None, "query"),
            P(None, "query", "slot", None, None),
            P(None, "query", "slot", None, None),
            P(None, "query", "slot"),
            P("query", None),
            P("query"),
            P("query"),
            P("query", None),
            P("query"),
            P("query"),
            P("query"),
            P("query", None),
            P("query"),
            P("query", None),
            P("query"),
            P("query"),
            P("query"),
            P("query", None),
            P("query", None),
        ),
        check_vma=False,
    )
```

```python
import functools

import jax
import jax.numpy as jnp
from jax import lax
from jax.experimental import pallas as pl
from jax.experimental.pallas import tpu as pltpu
from jax.sharding import PartitionSpec as P

HEAD = 64
NEG_FILL = -1e30
NORM_EPS = 1e-12
TOP_PRECISION = lax.Precision.HIGHEST
ROOT_HALF = 0.7071067811865476
DENSITY_SCALE = 0.3989422804014327
BF = jnp.bfloat16
F32 = jnp.float32


def times_right(left_side, right_side):
    return lax.dot_general(
        left_side,
        right_side,
        (((left_side.ndim - 1,), (0,)), ((), ())),
        preferred_element_type=F32,
    )


def times_transposed(left_side, right_side):
    return lax.dot_general(
        left_side,
        right_side,
        (((left_side.ndim - 1,), (1,)), ((), ())),
        preferred_element_type=F32,
    )


def gelu_value(inner_pre):
    return 0.5 * inner_pre * (1.0 + lax.erf(inner_pre * ROOT_HALF))


def gelu_slope(inner_pre):
    return (
        0.5 * (1.0 + lax.erf(inner_pre * ROOT_HALF))
        + inner_pre * jnp.exp(-0.5 * inner_pre * inner_pre) * DENSITY_SCALE
    )


def rounded_up(value, multiple):
    return -(-value // multiple) * multiple


def col_iota(shape, dim):
    return lax.broadcasted_iota(jnp.int32, shape, dim)


def dot_nn(a, b):
    return lax.dot_general(a, b, (((1,), (0,)), ((), ())), preferred_element_type=F32)


def dot_nt(a, b):
    return lax.dot_general(a, b, (((1,), (1,)), ((), ())), preferred_element_type=F32)


def dot_tn(a, b):
    return lax.dot_general(a, b, (((0,), (0,)), ((), ())), preferred_element_type=F32)


def dot_full(a, b, dims):
    return lax.dot_general(
        a, b, (dims, ((), ())), preferred_element_type=F32, precision=TOP_PRECISION
    )


def split_three(value):
    high = value.astype(BF).astype(F32)
    rest = value - high
    middle = rest.astype(BF).astype(F32)
    return high, middle, rest - middle


def pack_lanes(columns, rows):
    lane = col_iota((rows, 128), 1)
    out = jnp.zeros((rows, 128), F32)
    for k, column in enumerate(columns):
        out = jnp.where(lane == k, column, out)
    return out


def lane_sum(value, first, count):
    lane = col_iota(value.shape, 1)
    keep = (lane >= first) & (lane < first + count)
    return jnp.sum(jnp.where(keep, value, 0.0), axis=1, keepdims=True)


def full_spec(array):
    ndim = len(array.shape)
    return pl.BlockSpec(array.shape, lambda *_: (0,) * ndim)


ANY_SPEC = pl.BlockSpec(memory_space=pl.ANY)
SMEM_SPEC = pl.BlockSpec(memory_space=pltpu.SMEM)
VMEM_SPEC = pl.BlockSpec(memory_space=pltpu.VMEM)


V_BQ, V_BV, V_BO, V_G1, V_S1, V_BF, V_G2, V_S2, V_BI = range(9)


def forward_kernel(
    micro,
    own_rows,
    token_ref,
    mask_ref,
    hidden_ref,
    vec_ref,
    wqkv_hbm,
    wout_hbm,
    win_hbm,
    wffn_hbm,
    layer_ref,
    kv_ref,
    picked_ref,
    rows_ref,
    norm_ref,
    inv_ref,
    wqkv,
    wout,
    win,
    wffn,
    united,
    context,
    first_out,
    first_low,
    acc,
    norm_one,
    norm_two,
    inverse,
    sems,
):
    tokens, width = hidden_ref.shape
    seq_len = tokens // micro
    inner = win.shape[1]
    score_scale = HEAD ** (-0.5)
    copies = [
        pltpu.make_async_copy(src, dst, sems.at[k])
        for k, (src, dst) in enumerate(
            ((wqkv_hbm, wqkv), (wout_hbm, wout), (win_hbm, win), (wffn_hbm, wffn))
        )
    ]
    for copy in copies:
        copy.start()
    half = width // 2
    copies[0].wait()
    for part in range(6):
        cols = slice(part * half, (part + 1) * half)
        out = dot_nn(hidden_ref[...], wqkv[:, cols])
        sub = slice((part % 2) * half, (part % 2 + 1) * half)
        if part < 2:
            out = out + vec_ref[V_BQ : V_BQ + 1, sub]
        elif part >= 4:
            out = out + vec_ref[V_BV : V_BV + 1, sub]
        united[:, cols] = out.astype(BF)

    first_head = col_iota((seq_len, 128), 1) < HEAD

    def attend(pair, carry):
        col = pl.multiple_of(pair * 128, 128)
        for b in range(micro):
            rows = slice(b * seq_len, (b + 1) * seq_len)
            query = united[rows, pl.ds(col, 128)]
            key = united[rows, pl.ds(width + col, 128)]
            value = united[rows, pl.ds(2 * width + col, 128)]
            ok = mask_ref[b : b + 1, :] > 0
            parts = []
            for h in range(2):
                mine = first_head if h == 0 else ~first_head
                scores = dot_nt(jnp.where(mine, query, jnp.zeros_like(query)), key) * score_scale
                scores = jnp.where(ok, scores, NEG_FILL)
                powers = jnp.exp(scores - jnp.max(scores, axis=1, keepdims=True))
                probs = powers / jnp.sum(powers, axis=1, keepdims=True)
                parts.append(dot_nn(probs.astype(BF), value))
            context[rows, pl.ds(col, 128)] = jnp.where(first_head, parts[0], parts[1]).astype(BF)
        return carry

    lax.fori_loop(0, width // 128, attend, 0)
    kv_ref[...] = united[:, width:]

    copies[1].wait()
    acc[...] = dot_nn(context[...], wout[...])
    step_rows = 32

    def norm_first(step, carry):
        rows = pl.ds(pl.multiple_of(step * step_rows, step_rows), step_rows)
        summed = hidden_ref[rows, :].astype(F32) + (acc[rows, :] + vec_ref[V_BO : V_BO + 1, :])
        centre = summed - jnp.mean(summed, axis=1, keepdims=True)
        inv = lax.rsqrt(jnp.mean(centre * centre, axis=1, keepdims=True) + NORM_EPS)
        normed = centre * inv
        out = normed * vec_ref[V_G1 : V_G1 + 1, :] + vec_ref[V_S1 : V_S1 + 1, :]
        norm_one[rows, :] = normed
        first_out[rows, :] = out
        first_low[rows, :] = out.astype(BF)
        inverse[rows, 0:128] = jnp.broadcast_to(inv, (step_rows, 128))
        return carry

    lax.fori_loop(0, tokens // step_rows, norm_first, 0)
    copies[2].wait()
    copies[3].wait()
    acc[...] = first_out[...] + vec_ref[V_BF : V_BF + 1, :]
    per_row = width // half

    def feed(step, carry):
        cols = pl.ds(pl.multiple_of(step * half, half), half)
        bias = vec_ref[pl.ds(V_BI + step, 1), :]
        pre = dot_nn(first_low[...], win[:, cols]) + bias[:, :half]
        active = (0.5 * pre * (1.0 + lax.erf(pre * ROOT_HALF))).astype(BF)
        acc[...] += dot_nn(active, wffn[cols, :])
        return carry

    lax.fori_loop(0, inner // half, feed, 0)

    def norm_second(step, carry):
        rows = pl.ds(pl.multiple_of(step * step_rows, step_rows), step_rows)
        summed = acc[rows, :]
        centre = summed - jnp.mean(summed, axis=1, keepdims=True)
        inv = lax.rsqrt(jnp.mean(centre * centre, axis=1, keepdims=True) + NORM_EPS)
        normed = centre * inv
        out = normed * vec_ref[V_G2 : V_G2 + 1, :] + vec_ref[V_S2 : V_S2 + 1, :]
        norm_two[rows, :] = normed
        layer_ref[rows, :] = out.astype(BF)
        inverse[rows, 128:256] = jnp.broadcast_to(inv, (step_rows, 128))
        return carry

    lax.fori_loop(0, tokens // step_rows, norm_second, 0)

    n_rows = token_ref.shape[0]
    place = token_ref[...] == col_iota((n_rows, tokens), 1)
    place_low = jnp.where(place, 1.0, 0.0).astype(BF)
    second_rows = dot_nn(place_low, layer_ref[...]).astype(BF)
    rows_ref[0] = second_rows
    picked_ref[...] = second_rows[:own_rows]
    rows_ref[1] = dot_nn(place_low, first_low[...]).astype(BF)
    rows_ref[2] = dot_nn(place_low, context[...]).astype(BF)
    rows_ref[3] = dot_nn(place_low, hidden_ref[...]).astype(BF)
    rows_ref[4] = dot_nn(place_low, united[:, :width]).astype(BF)

    def take(value):
        high, middle, low = split_three(value)
        out = dot_nn(place_low, high.astype(BF)) + dot_nn(place_low, middle.astype(BF))
        return out + dot_nn(place_low, low.astype(BF))

    norm_ref[0] = take(norm_one[...])
    norm_ref[1] = take(norm_two[...])
    inv_ref[...] = take(inverse[...])


def forward(micro, own_rows, token_of, mask, hidden, vectors, w_qkv, w_out, w_in, w_ffn):
    tokens, width = hidden.shape
    inner = w_in.shape[1]
    n_rows = token_of.shape[0]
    out_shape = (
        jax.ShapeDtypeStruct((tokens, width), BF),
        jax.ShapeDtypeStruct((tokens, 2 * width), BF),
        jax.ShapeDtypeStruct((own_rows, width), BF),
        jax.ShapeDtypeStruct((5, n_rows, width), BF),
        jax.ShapeDtypeStruct((2, n_rows, width), F32),
        jax.ShapeDtypeStruct((n_rows, 256), F32),
    )
    return pl.pallas_call(
        functools.partial(forward_kernel, micro, own_rows),
        out_shape=out_shape,
        in_specs=[VMEM_SPEC] * 4 + [ANY_SPEC] * 4,
        out_specs=(VMEM_SPEC,) * 6,
        scratch_shapes=[
            pltpu.VMEM(w_qkv.shape, BF),
            pltpu.VMEM(w_out.shape, BF),
            pltpu.VMEM(w_in.shape, BF),
            pltpu.VMEM(w_ffn.shape, BF),
            pltpu.VMEM((tokens, 3 * width), BF),
            pltpu.VMEM((tokens, width), BF),
            pltpu.VMEM((tokens, width), F32),
            pltpu.VMEM((tokens, width), BF),
            pltpu.VMEM((tokens, width), F32),
            pltpu.VMEM((tokens, width), F32),
            pltpu.VMEM((tokens, width), F32),
            pltpu.VMEM((tokens, 256), F32),
            pltpu.SemaphoreType.DMA((4,)),
        ],
        compiler_params=pltpu.CompilerParams(vmem_limit_bytes=48 << 20),
        name="forward",
    )(token_of, mask, hidden, vectors, w_qkv, w_out, w_in, w_ffn)


def vocab_kernel(
    offsets, own_rows, q_ref, targets_ref, near_ref, far_ref, table_ref, out_ref, top, total, chosen, pull, picked, target
):
    step = pl.program_id(0)
    tile = table_ref.shape[0]
    width = table_ref.shape[1]
    n_q = len(offsets)
    q_me = q_ref[0]
    rows = n_q * own_rows

    @pl.when(step == 0)
    def _():
        for j, offset in enumerate(offsets):
            place = slice(j * own_rows, (j + 1) * own_rows)
            target[place, :] = targets_ref[q_me ^ offset]
            source = near_ref if j < n_q // 2 else far_ref
            picked[place, :] = source[j % (n_q // 2)]
        top[...] = jnp.full((rows, 1), NEG_FILL, F32)
        total[...] = jnp.zeros((rows, 1), F32)
        chosen[...] = jnp.zeros((rows, 1), F32)
        pull[...] = jnp.zeros((rows, width), F32)

    table = table_ref[...]
    logits = dot_nt(picked[...], table)
    hit = target[...] == col_iota((rows, tile), 1) + step * tile
    new_top = jnp.maximum(top[...], jnp.max(logits, axis=1, keepdims=True))
    scale = jnp.exp(top[...] - new_top)
    powers = jnp.exp(logits - new_top)
    total[...] = total[...] * scale + jnp.sum(powers, axis=1, keepdims=True)
    chosen[...] += jnp.sum(jnp.where(hit, logits, 0.0), axis=1, keepdims=True)
    others = jnp.where(hit, 0.0, powers).astype(BF)
    pull[...] = pull[...] * scale + dot_nn(others, table)
    top[...] = new_top

    @pl.when(step == pl.num_programs(0) - 1)
    def _():
        for j, offset in enumerate(offsets):
            place = slice(j * own_rows, (j + 1) * own_rows)
            columns = (
                split_three(top[place, :]) + split_three(total[place, :]) + split_three(chosen[place, :])
            )
            out_ref[q_me ^ offset, :, 0:width] = pull[place, :].astype(BF)
            out_ref[q_me ^ offset, :, width:] = pack_lanes(columns, own_rows).astype(BF)


def vocab_tile(vocab):
    return next(t for t in (768, 640, 512, 384, 320, 256, 192, 128) if vocab % t == 0)


def vocab_rows(offsets, q_me, targets_local, near, far, table):
    n_q = len(offsets)
    half_q, own_rows, width = near.shape
    vocab = table.shape[0]
    tile = vocab_tile(vocab)
    rows = n_q * own_rows
    return pl.pallas_call(
        functools.partial(vocab_kernel, offsets, own_rows),
        out_shape=jax.ShapeDtypeStruct((n_q, own_rows, width + 128), BF),
        grid=(vocab // tile,),
        in_specs=[
            SMEM_SPEC,
            full_spec(targets_local),
            full_spec(near),
            full_spec(far),
            pl.BlockSpec((tile, width), lambda i: (i, 0)),
        ],
        out_specs=pl.BlockSpec((n_q, own_rows, width + 128), lambda i: (0, 0, 0)),
        scratch_shapes=[
            pltpu.VMEM((rows, 1), F32),
            pltpu.VMEM((rows, 1), F32),
            pltpu.VMEM((rows, 1), F32),
            pltpu.VMEM((rows, width), F32),
            pltpu.VMEM((rows, width), BF),
            pltpu.VMEM((rows, 1), jnp.int32),
        ],
        compiler_params=pltpu.CompilerParams(vmem_limit_bytes=40 << 20),
        name="vocab",
    )(q_me, targets_local, near, far, table)


def combine_kernel(
    micro, masked, valid_ref, parts_ref, target_ref, second_ref, query_ref, wretr_ref, grad_ref, packed_ref, normal_ref
):
    n_q, own_rows, _ = parts_ref.shape
    n_rows, width = second_ref.shape
    rd = wretr_ref.shape[1]
    stats = [parts_ref[j, :, width:].astype(F32) for j in range(n_q)]
    tops = [lane_sum(s, 0, 3) for s in stats]
    totals = [lane_sum(s, 3, 3) for s in stats]
    chosen = functools.reduce(jnp.add, [lane_sum(s, 6, 3) for s in stats])
    top = functools.reduce(jnp.maximum, tops)
    scales = [jnp.exp(t - top) for t in tops]
    total = functools.reduce(jnp.add, [a * b for a, b in zip(scales, totals)])
    normal = top + jnp.log(total)
    row_ll = chosen - normal
    pull = jnp.zeros((own_rows, width), F32)
    target = jnp.zeros((own_rows, width), F32)
    for j in range(n_q):
        pull = pull + (scales[j] / total) * parts_ref[j, :, 0:width].astype(F32)
        target = target + target_ref[j].astype(F32)
    grad_ref[0:own_rows, :] = (pull + (jnp.exp(row_ll) - 1.0) * target) * (1.0 / masked)
    grad_ref[own_rows:, :] = dot_full(query_ref[...], wretr_ref[...].astype(F32), ((1,), (1,)))
    normal_ref[...] = jnp.zeros(normal_ref.shape, F32)
    normal_ref[0:own_rows, :] = jnp.broadcast_to(normal, (own_rows, 128))
    documents = dot_nn(second_ref[own_rows:, :], wretr_ref[...])
    retr = jnp.sum(documents * query_ref[...], axis=1, keepdims=True)
    row_id = col_iota((own_rows, 1), 0)
    tail = n_rows - own_rows
    out_id = col_iota((tail, 1), 0)
    likely = jnp.zeros((tail, 1), F32)
    valid = jnp.zeros((tail, 1), F32)
    for b in range(micro):
        mine = (row_id >= b * masked) & (row_id < (b + 1) * masked)
        mean = jnp.sum(jnp.where(mine, row_ll, 0.0), axis=0, keepdims=True) * (1.0 / masked)
        likely = jnp.where(out_id == b, mean, likely)
        valid = jnp.where(out_id == b, valid_ref[b].astype(F32), valid)
    packed_ref[:, 0:rd] = documents
    packed_ref[:, rd:] = pack_lanes((retr, likely, valid), tail)


def combine(micro, masked, valid, parts, targets_in, second_rows, query_full, w_retr):
    n_q, own_rows, _ = parts.shape
    n_rows, width = second_rows.shape
    tail = n_rows - own_rows
    return pl.pallas_call(
        functools.partial(combine_kernel, micro, masked),
        out_shape=(
            jax.ShapeDtypeStruct((n_rows, width), F32),
            jax.ShapeDtypeStruct((tail, w_retr.shape[1] + 128), F32),
            jax.ShapeDtypeStruct((n_rows, 128), F32),
        ),
        in_specs=[SMEM_SPEC] + [VMEM_SPEC] * 5,
        out_specs=(VMEM_SPEC,) * 3,
        name="combine",
    )(valid, parts, targets_in, second_rows, query_full, w_retr)


def norm_back(grad, normed, inverse, gain):
    scaled = grad * gain
    mean_grad = jnp.mean(scaled, axis=1, keepdims=True)
    mean_proj = jnp.mean(scaled * normed, axis=1, keepdims=True)
    return inverse * (scaled - mean_grad - normed * mean_proj)


def rows_back_kernel(
    grad_ref, norm_ref, inv_ref, slope_ref, vec_ref, wffn_hbm, win_hbm, branch_ref, first_ref, sum_ref, wffn, win, acc, sems
):
    copy_out = pltpu.make_async_copy(wffn_hbm, wffn, sems.at[0])
    copy_in = pltpu.make_async_copy(win_hbm, win, sems.at[1])
    copy_out.start()
    copy_in.start()
    inner, width = wffn.shape
    branch = norm_back(
        grad_ref[...], norm_ref[1], inv_ref[:, 128:129], vec_ref[V_G2 : V_G2 + 1, :]
    )
    branch_ref[...] = branch
    branch_low = branch.astype(BF)
    acc[...] = branch
    copy_out.wait()
    copy_in.wait()
    chunk = width // 2

    def feed(step, carry):
        cols = pl.ds(pl.multiple_of(step * chunk, chunk), chunk)
        back = dot_nt(branch_low, wffn[cols, :]) * slope_ref[0, :, cols].astype(F32)
        acc[...] += dot_nt(back.astype(BF), win[:, cols])
        return carry

    lax.fori_loop(0, inner // chunk, feed, 0)
    first = acc[...]
    first_ref[...] = first
    sum_ref[...] = norm_back(first, norm_ref[0], inv_ref[:, 0:1], vec_ref[V_G1 : V_G1 + 1, :])


def rows_back(grad_rows, norms, inverses, slopes, vectors, w_ffn, w_in):
    n_rows, width = grad_rows.shape
    shape = jax.ShapeDtypeStruct((n_rows, width), F32)
    slope_spec = pl.BlockSpec((1,) + slopes.shape[1:], lambda i: (0, 0, 0))
    return pl.pallas_call(
        rows_back_kernel,
        out_shape=(shape,) * 3,
        grid=(1,),
        in_specs=[full_spec(grad_rows), full_spec(norms), full_spec(inverses), slope_spec, full_spec(vectors)]
        + [ANY_SPEC] * 2,
        out_specs=(full_spec(shape),) * 3,
        scratch_shapes=[
            pltpu.VMEM(w_ffn.shape, BF),
            pltpu.VMEM(w_in.shape, BF),
            pltpu.VMEM((n_rows, width), F32),
            pltpu.SemaphoreType.DMA((2,)),
        ],
        compiler_params=pltpu.CompilerParams(vmem_limit_bytes=32 << 20),
        name="rows_back",
    )(grad_rows, norms, inverses, slopes, vectors, w_ffn, w_in)


def grads_kernel(
    micro,
    masked,
    n_q,
    n_s,
    x_split,
    ids_ref,
    *refs,
):
    packs = refs[:n_s]
    (
        grad_ref,
        branch_ref,
        first_ref,
        sum_ref,
        norm_ref,
        rows_ref,
        kv_ref,
        hidden_ref,
        wout_ref,
        query_ref,
        normal_ref,
        mask_ref,
        ea_ref,
        eb_ref,
        pay_ref,
        kvg_ref,
        gq_ref,
        scaled_ref,
        slots_ref,
        pay,
        gctx,
        att,
    ) = refs[n_s:]
    q_me, s_me = ids_ref[0], ids_ref[1]
    core_me, x_me = s_me & 1, s_me >> 1
    n_rows, width = grad_ref.shape
    own_rows = micro * masked
    tail = n_rows - own_rows
    tokens = hidden_ref.shape[0]
    seq_len = tokens // micro
    rd = query_ref.shape[1]
    score_scale = HEAD ** (-0.5)

    lane = col_iota((tail, 128), 1)
    retr = jnp.zeros((tail, 128), F32)
    likely = jnp.zeros((tail, 128), F32)
    valid = jnp.zeros((tail, 128), F32)
    for k, ref in enumerate(packs):
        at = lane == (s_me ^ k)
        retr = jnp.where(at, ref[:, rd : rd + 1], retr)
        likely = jnp.where(at, ref[:, rd + 1 : rd + 2], likely)
        valid = jnp.where(at, ref[:, rd + 2 : rd + 3], valid)
    slot_ok = valid > 0

    def log_sum(score):
        top = jnp.max(score, axis=1, keepdims=True)
        return top + jnp.log(jnp.sum(jnp.exp(score - top), axis=1, keepdims=True))

    score = jnp.where(slot_ok, retr, NEG_FILL)
    joint = jnp.where(slot_ok, retr + likely, NEG_FILL)
    prior_lse = log_sum(score)
    joint_lse = log_sum(joint)
    prior = jnp.where(slot_ok, jnp.exp(score - prior_lse), 0.0)
    post = jnp.where(slot_ok, jnp.exp(joint - joint_lse), 0.0)
    grad_score = prior - post
    slots_ref[0] = jnp.broadcast_to(joint_lse - prior_lse, (tail, 128))
    query_grad = jnp.zeros((tail, rd), F32)
    for k, ref in enumerate(packs):
        gs = jnp.sum(jnp.where(lane == (s_me ^ k), grad_score, 0.0), axis=1, keepdims=True)
        query_grad = query_grad + gs * ref[:, 0:rd]
    slots_ref[1] = query_grad
    own_post = jnp.sum(jnp.where(lane == s_me, post, 0.0), axis=1, keepdims=True)
    own_score = jnp.sum(jnp.where(lane == s_me, grad_score, 0.0), axis=1, keepdims=True)
    row_id = col_iota((n_rows, 1), 0)
    scale = jnp.zeros((n_rows, 1), F32)
    for b in range(micro):
        mine = (row_id >= b * masked) & (row_id < (b + 1) * masked)
        scale = jnp.where(mine, own_post[b : b + 1], scale)
        scale = jnp.where(row_id == own_rows + b, own_score[b : b + 1], scale)

    scaled_one = sum_ref[...] * scale
    scaled_ref[...] = scaled_one
    att[...] = scaled_one.astype(BF)
    gctx[...] = dot_nt(att[...], wout_ref[...]).astype(BF)
    first_head = col_iota((1, 128), 1) < HEAD

    def attend(pair, carry):
        col = pl.multiple_of(pair * 128, 128)
        query = rows_ref[4, :, pl.ds(col, 128)]
        up = gctx[:, pl.ds(col, 128)]
        gq = jnp.zeros((n_rows, 128), F32)
        zero = jnp.zeros_like(query)
        for b in range(micro):
            rows = slice(b * seq_len, (b + 1) * seq_len)
            key = kv_ref[rows, pl.ds(col, 128)]
            value = kv_ref[rows, pl.ds(width + col, 128)]
            ok = mask_ref[b : b + 1, :] > 0
            mine = ((row_id >= b * masked) & (row_id < (b + 1) * masked)) | (
                row_id == own_rows + b
            )
            gk = jnp.zeros((seq_len, 128), F32)
            gv = jnp.zeros((seq_len, 128), F32)
            for h in range(2):
                head = first_head if h == 0 else ~first_head
                query_h = jnp.where(head, query, zero)
                up_h = jnp.where(head, up, zero)
                scores = dot_nt(query_h, key) * score_scale
                scores = jnp.where(ok, scores, NEG_FILL)
                powers = jnp.exp(scores - jnp.max(scores, axis=1, keepdims=True))
                probs = powers / jnp.sum(powers, axis=1, keepdims=True)
                probs = jnp.where(mine, probs, 0.0)
                grad_probs = dot_nt(up_h, value)
                delta = jnp.sum(probs * grad_probs, axis=1, keepdims=True)
                ds = (probs * (grad_probs - delta)).astype(BF)
                gq = gq + jnp.where(head, dot_nn(ds, key), 0.0)
                gk = gk + dot_tn(ds, query_h)
                gv = gv + dot_tn(probs.astype(BF), up_h)
            kvg_ref[rows, pl.ds(col, 128)] = (gk * score_scale).astype(BF)
            kvg_ref[rows, pl.ds(width + col, 128)] = gv.astype(BF)
        gq_ref[:, pl.ds(col, 128)] = (gq * score_scale).astype(BF)
        return carry

    lax.fori_loop(0, width // 128, attend, 0)

    half = width // 2
    half_q = n_q // 2
    part = width // (n_q * x_split)
    panels = (
        (ea_ref, 0, rows_ref.at[2], att, 0),
        (ea_ref, 1, rows_ref.at[3], gq_ref, 0),
        (eb_ref, 0, hidden_ref, kvg_ref, 0),
        (eb_ref, 1, hidden_ref, kvg_ref, width),
    )
    chunk = 384
    for out_ref, panel, left, right, first_col in panels:
        for core in range(2):
            jc = core ^ core_me
            grad_cols = slice(first_col + core * half, first_col + (core + 1) * half)
            for c in range(width // chunk):
                out = dot_tn(left[:, c * chunk : (c + 1) * chunk], right[:, grad_cols])
                for block in range(chunk // part):
                    a = c * (chunk // part) + block
                    jq = (a // x_split) ^ q_me
                    jx = (a % x_split) ^ x_me if x_split > 1 else 0
                    jy, jz = jq & 1, jq >> 1
                    if out_ref is ea_ref:
                        index = ((jc * x_split + jx) * 2 + jy) * half_q + jz
                    else:
                        index = ((jc * 2 + jy) * x_split + jx) * half_q + jz
                    out_ref[index, panel * part : (panel + 1) * part, :] = out[
                        block * part : (block + 1) * part
                    ].astype(BF)

    pay[...] = jnp.zeros(pay.shape, F32)
    pay[0:n_rows, 0:width] = branch_ref[...] * scale
    columns = split_three(scale) + split_three(normal_ref[:, 0:1])
    pay[0:n_rows, width:] = pack_lanes(columns, n_rows)
    r_cls = own_rows + micro
    for b in range(micro):
        row = slice(r_cls + b, r_cls + b + 1)
        pay[row, 0:width] = rows_ref[0, own_rows : own_rows + 8, :].astype(F32)[b : b + 1]
        pay[row, width:] = query_ref[b : b + 1, :]
    scaled_two = grad_ref[...] * scale
    scaled_first = first_ref[...] * scale
    sums = (
        jnp.sum(gq_ref[...].astype(F32), axis=0, keepdims=True),
        jnp.sum(kvg_ref[:, width:].astype(F32), axis=0, keepdims=True),
        jnp.sum(att[...].astype(F32), axis=0, keepdims=True),
        jnp.sum(scaled_first * norm_ref[0], axis=0, keepdims=True),
        jnp.sum(scaled_first, axis=0, keepdims=True),
        jnp.sum(scaled_two * norm_ref[1], axis=0, keepdims=True),
        jnp.sum(scaled_two, axis=0, keepdims=True),
    )
    for k, value in enumerate(sums):
        row = r_cls + micro + k
        pay[row : row + 1, 0:width] = value
        pay[row : row + 1, width:] = jnp.zeros((1, 128), F32)
    pay_ref[...] = pay[...].astype(BF)


N_SUMS = 7


def grads(micro, masked, n_q, n_s, x_split, ids, packs, operands):
    grad_rows, kv, hidden = operands[0], operands[6], operands[7]
    n_rows, width = grad_rows.shape
    tail = n_rows - micro * masked
    pay_rows = rounded_up(max(n_rows, micro * masked + 2 * micro + N_SUMS), 8)
    part = width // (n_q * x_split)
    blocks = 2 * x_split * n_q
    return pl.pallas_call(
        functools.partial(grads_kernel, micro, masked, n_q, n_s, x_split),
        out_shape=(
            jax.ShapeDtypeStruct((blocks, 2 * part, width // 2), BF),
            jax.ShapeDtypeStruct((blocks, 2 * part, width // 2), BF),
            jax.ShapeDtypeStruct((pay_rows, width + 128), BF),
            jax.ShapeDtypeStruct(kv.shape, BF),
            jax.ShapeDtypeStruct((n_rows, width), BF),
            jax.ShapeDtypeStruct((n_rows, width), F32),
            jax.ShapeDtypeStruct((2, tail, 128), F32),
        ),
        in_specs=[SMEM_SPEC] + [VMEM_SPEC] * (n_s + len(operands)),
        out_specs=(VMEM_SPEC,) * 7,
        scratch_shapes=[
            pltpu.VMEM((pay_rows, width + 128), F32),
            pltpu.VMEM((n_rows, width), BF),
            pltpu.VMEM((n_rows, width), BF),
        ],
        compiler_params=pltpu.CompilerParams(vmem_limit_bytes=40 << 20),
        name="grads",
    )(ids, *packs, *operands)


def feed_kernel(
    micro,
    masked,
    n_rows,
    x_split,
    ids_ref,
    pay_near,
    pay_far,
    first_near,
    first_far,
    active_ref,
    slope_ref,
    wffn_hbm,
    out_ref,
    info_ref,
    wffn,
    branch,
    first_own,
    sums,
    sems,
):
    copy = pltpu.make_async_copy(wffn_hbm, wffn, sems.at[0])
    copy.start()
    q_me, s_me = ids_ref[0], ids_ref[1]
    core_me, x_me = s_me & 1, s_me >> 1
    half_q = pay_near.shape[0]
    n_q = 2 * half_q
    inner, width = wffn.shape
    half = width // 2
    own_rows = micro * masked
    r_cls = own_rows + micro
    rows_in, rows_out = width // n_q, inner // n_q
    part_in, part_out = rows_in // x_split, rows_out // x_split
    small_at = part_in * (inner // width) + part_out
    small_len = out_ref.shape[1] - small_at
    select = jnp.where(
        col_iota((width, rows_in), 0) == col_iota((width, rows_in), 1) + q_me * rows_in, 1.0, 0.0
    ).astype(BF)
    keep = col_iota((n_rows, 1), 0) < r_cls
    totals = jnp.zeros((8, width), F32)
    vec_id = col_iota((8, 1), 0)
    retr = jnp.zeros((rows_in, 128), F32)
    for j in range(n_q):
        pay = (pay_near if j < half_q else pay_far).at[j % half_q]
        place = slice(j * n_rows, (j + 1) * n_rows)
        rows = jnp.where(keep, pay[0:n_rows, 0:width].astype(F32), 0.0)
        branch[place, :] = rows.astype(BF)
        first = (first_near if j < half_q else first_far)[j % half_q]
        first_own[place, :] = dot_nn(first, select).astype(BF)
        info = pay[0:n_rows, width:].astype(F32)
        scale = lane_sum(info, 0, 3)
        normal = lane_sum(info, 3, 3)
        info_ref[j] = pack_lanes((scale * (1.0 / masked), normal), n_rows)[0:own_rows]
        tail = pay[own_rows:, :].astype(F32)
        own_sum = jnp.sum(rows, axis=0, keepdims=True)
        for k in range(N_SUMS):
            row = micro + micro + k
            totals = totals + jnp.where(vec_id == k, tail[row : row + 1, 0:width], 0.0)
        totals = totals + jnp.where(vec_id == N_SUMS, own_sum, 0.0)
        for b in range(micro):
            first_token = tail[micro + b : micro + b + 1, 0:width].astype(BF)
            column = dot_nn(first_token, select)
            row = tail[micro + b : micro + b + 1, width:] * scale[own_rows + b : own_rows + b + 1]
            retr = retr + dot_full(column, row, ((0,), (0,)))
    copy.wait()
    out_ref[:, small_at:, :] = jnp.zeros((2 * x_split, small_len, half), BF)
    chunks = inner // half

    def index_of(core, x):
        jc = core ^ core_me
        return jc * x_split + ((x ^ x_me) if x_split > 1 else 0)

    for c in range(chunks):
        cols = slice(c * half, (c + 1) * half)
        back = dot_nt(branch[...], wffn[cols, :]) * slope_ref[:, cols].astype(F32)
        back = back.astype(BF)
        sums[c : c + 1, :] = jnp.sum(back.astype(F32), axis=0, keepdims=True)
        in_part = dot_tn(first_own[...], back)
        core, p = c // (chunks // 2), c % (chunks // 2)
        for x in range(x_split):
            out_ref[index_of(core, x), p * part_in : (p + 1) * part_in, :] = in_part[
                x * part_in : (x + 1) * part_in
            ].astype(BF)
    if rows_out % 128 == 0:
        active_own = active_ref[:, pl.ds(pl.multiple_of(q_me * rows_out, 128), rows_out)]
    else:
        pick_out = jnp.where(
            col_iota((inner, rows_out), 0) == col_iota((inner, rows_out), 1) + q_me * rows_out,
            1.0,
            0.0,
        ).astype(BF)
        active_own = dot_nn(active_ref[...], pick_out).astype(BF)
    for core in range(2):
        out_part = dot_tn(active_own, branch[:, core * half : (core + 1) * half])
        for x in range(x_split):
            at = small_at - part_out
            out_ref[index_of(core, x), at : at + part_out, :] = out_part[
                x * part_out : (x + 1) * part_out
            ].astype(BF)
    index = index_of(0, 0)
    third = rows_in // 3
    for k in range(3):
        out_ref[index, small_at : small_at + third, k * 128 : (k + 1) * 128] = retr[
            k * third : (k + 1) * third
        ].astype(BF)
    at = small_at + third
    out_ref[index, at : at + 8, :] = sums[...].astype(BF)
    out_ref[index, at + 8 : at + 16, :] = totals[:, 0:half].astype(BF)
    out_ref[index, at + 16 : at + 24, :] = totals[:, half:].astype(BF)


def feed_grads(micro, masked, x_split, ids, pay_near, pay_far, first_near, first_far, active, slope, w_ffn):
    half_q, n_rows, width = first_near.shape
    n_q = 2 * half_q
    inner = w_ffn.shape[0]
    rows_in, rows_out = width // n_q, inner // n_q
    length = (rows_in * (inner // width) + rows_out) // x_split + rows_in // 3 + 24
    return pl.pallas_call(
        functools.partial(feed_kernel, micro, masked, n_rows, x_split),
        out_shape=(
            jax.ShapeDtypeStruct((2 * x_split, length, width // 2), BF),
            jax.ShapeDtypeStruct((n_q, micro * masked, 128), F32),
        ),
        in_specs=[SMEM_SPEC] + [VMEM_SPEC] * 6 + [ANY_SPEC],
        out_specs=(VMEM_SPEC,) * 2,
        scratch_shapes=[
            pltpu.VMEM(w_ffn.shape, BF),
            pltpu.VMEM((n_q * n_rows, width), BF),
            pltpu.VMEM((n_q * n_rows, rows_in), BF),
            pltpu.VMEM((8, width // 2), F32),
            pltpu.SemaphoreType.DMA((1,)),
        ],
        compiler_params=pltpu.CompilerParams(vmem_limit_bytes=56 << 20),
        name="feed_grads",
    )(ids, pay_near, pay_far, first_near, first_far, active, slope, w_ffn)


def table_kernel(first_tile, info_ref, target_ref, picked_ref, table_ref, *rest):
    out_ref = rest[-1]
    tile = table_ref.shape[0]
    rows = picked_ref.shape[0]
    step = 1280 if rows % 1280 == 0 else rows
    base = (pl.program_id(0) + first_tile) * tile
    table = table_ref[...]
    total = None
    for c in range(rows // step):
        cols = slice(c * step, (c + 1) * step)
        picked = picked_ref[cols, :]
        logits = dot_nt(table, picked)
        hit = target_ref[0:1, cols] == col_iota((tile, step), 0) + base
        grad = jnp.exp(logits - info_ref[1:2, cols]) - jnp.where(hit, 1.0, 0.0)
        grad = (grad * info_ref[0:1, cols]).astype(BF)
        part = dot_nn(grad, picked)
        total = part if total is None else total + part
    out_ref[...] = total


def table_grad_part(first_tile, n_tiles, tile, info, targets, picked_all, table, before):
    vocab, width = table.shape
    once = pl.Buffered(1)
    extra = [] if before is None else [before]
    return pl.pallas_call(
        functools.partial(table_kernel, first_tile),
        out_shape=jax.ShapeDtypeStruct((vocab, width), F32),
        grid=(n_tiles,),
        in_specs=[
            pl.BlockSpec(info.shape, lambda i: (0, 0), pipeline_mode=once),
            pl.BlockSpec(targets.shape, lambda i: (0, 0), pipeline_mode=once),
            pl.BlockSpec(picked_all.shape, lambda i: (0, 0), pipeline_mode=once),
            pl.BlockSpec((tile, width), lambda i: (i + first_tile, 0)),
        ]
        + [ANY_SPEC] * len(extra),
        out_specs=pl.BlockSpec((tile, width), lambda i: (i + first_tile, 0)),
        input_output_aliases={} if before is None else {4: 0},
        compiler_params=pltpu.CompilerParams(vmem_limit_bytes=48 << 20),
        cost_estimate=pl.CostEstimate(
            flops=4 * n_tiles * tile * width * picked_all.shape[0],
            bytes_accessed=6 * n_tiles * tile * width + 2 * picked_all.size,
            transcendentals=n_tiles * tile * picked_all.shape[0],
        ),
        name="table_grad",
    )(info, targets, picked_all, table, *extra)


def assemble_kernel(
    n_q, x_split, inner, ids_ref, own_ref, other_ref, wout_ref, wqkv_ref, win_ref, wffn_ref, wretr_ref, vec_ref
):
    s_me = ids_ref[1]
    core_me, x_me = s_me & 1, s_me >> 1
    half = own_ref.shape[2]
    width = 2 * half
    rows_in, rows_out = width // n_q, inner // n_q
    part_in, part_out = rows_in // x_split, rows_out // x_split
    third = rows_in // 3
    panels = inner // width
    for jc, source in enumerate((own_ref, other_ref)):
        core = core_me ^ jc
        for jx in range(x_split):
            x = (x_me ^ jx) if x_split > 1 else 0
            piece = source.at[jx]
            rows = pl.ds(pl.multiple_of(x * part_in, 8), part_in)

            def cols(start):
                return pl.ds(pl.multiple_of(start, 128), half)

            def load(start, length):
                return piece[start : start + length, :].astype(F32)

            wout_ref[rows, cols(core * half)] = load(0, part_in)
            for k in range(3):
                wqkv_ref[rows, cols(k * width + core * half)] = load((k + 1) * part_in, part_in)
            at = 4 * part_in
            for p in range(panels):
                win_ref[rows, cols((core * panels + p) * half)] = load(at + p * part_in, part_in)
            at = at + panels * part_in
            out_rows = pl.ds(pl.multiple_of(x * part_out, 8), part_out)
            wffn_ref[out_rows, cols(core * half)] = load(at, part_out)
            at = at + part_out

            @pl.when((core == 0) & (x == 0))
            def _():
                for k in range(3):
                    wretr_ref[k * third : (k + 1) * third, :] = piece[
                        at : at + third, k * 128 : (k + 1) * 128
                    ].astype(F32)
                vec_ref[...] = load(at + third, 24)


def assemble(n_q, x_split, inner, rd, ids, own, other):
    half = own.shape[2]
    width = 2 * half
    rows_in, rows_out = width // n_q, inner // n_q
    return pl.pallas_call(
        functools.partial(assemble_kernel, n_q, x_split, inner),
        out_shape=(
            jax.ShapeDtypeStruct((rows_in, width), F32),
            jax.ShapeDtypeStruct((rows_in, 3 * width), F32),
            jax.ShapeDtypeStruct((rows_in, inner), F32),
            jax.ShapeDtypeStruct((rows_out, width), F32),
            jax.ShapeDtypeStruct((rows_in, rd), F32),
            jax.ShapeDtypeStruct((24, half), F32),
        ),
        in_specs=[SMEM_SPEC] + [VMEM_SPEC] * 2,
        out_specs=(VMEM_SPEC,) * 6,
        name="assemble",
    )(ids, own, other)


def per_device(
    n_q,
    n_s,
    hidden_in,
    token_mask,
    masked_pos,
    targets,
    slot_mask,
    query_embed,
    w_qkv,
    b_query,
    b_value,
    w_out,
    b_out,
    gain_first,
    shift_first,
    w_in,
    b_in,
    w_ffn_out,
    b_ffn_out,
    gain_second,
    shift_second,
    w_retr,
    word_table,
):
    micro, _, _, seq_len, width = hidden_in.shape
    masked = masked_pos.shape[-1]
    tokens = micro * seq_len
    inner = w_in.shape[1]
    rd = w_retr.shape[1]
    vocab_own = word_table.shape[0]
    own_rows = micro * masked
    n_rows = rounded_up(own_rows + micro, 16)
    q_me = lax.axis_index("query")
    s_me = lax.axis_index("slot")
    ids = jnp.stack([q_me, s_me]).astype(jnp.int32)
    n_x = n_s // 2
    half_q = n_q // 2
    x_split = n_x if (width // n_q) % (8 * n_x) == 0 else 1
    offsets = [2 * k + j for j in (0, 1) for k in range(half_q)]
    q_order = q_me ^ jnp.array(offsets, jnp.int32)

    def over_query(value, offset):
        return lax.ppermute(value, "query", [(i, i ^ offset) for i in range(n_q)])

    def over_slot(value, offset):
        return lax.ppermute(value, "slot", [(i, i ^ offset) for i in range(n_s)])

    def gather_query(value):
        near = jnp.stack([value] + [over_query(value, 2 * k) for k in range(1, half_q)])
        return near, over_query(near, 1)

    slot_targets = targets[:, :, 0, :].transpose(1, 0, 2).reshape(n_q, own_rows)
    local_targets = slot_targets - q_me * vocab_own
    target_hit = local_targets.reshape(-1, 1) == lax.iota(jnp.int32, vocab_own)[None, :]
    target_part = times_right(target_hit.astype(BF), word_table).astype(BF)
    target_parts = lax.all_to_all(target_part.reshape(n_q, own_rows, width), "query", 0, 0)

    hidden = hidden_in.reshape(tokens, width)
    mask = token_mask.reshape(micro, seq_len)
    vectors = jnp.concatenate(
        [b_query, b_value, b_out, gain_first, shift_first, b_ffn_out, gain_second, shift_second]
    ).astype(F32)
    bias_in = jnp.pad(b_in.astype(F32).reshape(-1, width // 2), ((0, 0), (0, width // 2)))
    vectors = jnp.concatenate([vectors.reshape(-1, width), bias_in], axis=0)
    first_token = jnp.arange(micro, dtype=jnp.int32)[:, None] * seq_len
    token_of = jnp.concatenate(
        [
            (masked_pos.reshape(micro, masked) + first_token).reshape(-1),
            first_token.reshape(-1),
            jnp.zeros((n_rows - own_rows - micro,), jnp.int32),
        ]
    ).reshape(n_rows, 1)
    layer_out, kv, picked, rows, norms, inverses = forward(
        micro, own_rows, token_of, mask, hidden, vectors, w_qkv, w_out, w_in, w_ffn_out
    )

    near, far = gather_query(picked)
    payload = vocab_rows(offsets, ids, local_targets[:, :, None], near, far, word_table)
    parts = lax.all_to_all(payload, "query", 0, 0)

    first_near, first_far = gather_query(rows[1])
    first_q = jnp.concatenate([first_near, first_far], axis=0).reshape(n_q * n_rows, width)
    inner_q = times_right(first_q, w_in) + b_in.astype(F32)
    active_q = gelu_value(inner_q).astype(BF)
    slope_q = gelu_slope(inner_q).astype(BF)

    query_full = lax.all_gather(query_embed, "slot", axis=2, tiled=True)[:, 0].astype(F32)
    query_full = jnp.pad(query_full, ((0, n_rows - own_rows - micro), (0, 0)))
    valid = slot_mask.reshape(micro)
    grad_rows, packed, normal = combine(
        micro, masked, valid, parts, target_parts, rows[0], query_full, w_retr
    )
    packs = [packed] + [over_slot(packed, k) for k in range(1, n_s)]
    branch, first_grad, sum_one = rows_back(
        grad_rows, norms, inverses, slope_q.reshape(n_q, n_rows, inner), vectors, w_ffn_out, w_in
    )
    ea, eb, pay, kv_grad, query_low, scaled_one, slots_out = grads(
        micro,
        masked,
        n_q,
        n_s,
        x_split,
        ids,
        packs,
        (
            grad_rows,
            branch,
            first_grad,
            sum_one,
            norms,
            rows,
            kv,
            hidden,
            w_out,
            query_full,
            normal,
            mask,
        ),
    )
    marginal = slots_out[0, :micro, :1]
    part = query_embed.shape[2]
    query_grad = lax.dynamic_slice_in_dim(slots_out[1, :micro], s_me * part, part, 1)[:, None, :]

    def step(value, dim, permute):
        out = lax.index_in_dim(value, 0, dim, keepdims=False)
        for j in range(1, value.shape[dim]):
            sent = lax.index_in_dim(value, j, dim, keepdims=False).astype(BF)
            out = out.astype(F32) + permute(sent, j).astype(F32)
        return out

    block = ea.shape[1:]
    sum_a = step(ea.reshape((2, x_split, 2, half_q) + block), 0, lambda v, j: over_slot(v, 1))
    sum_b = step(eb.reshape((2, 2, x_split, half_q) + block), 0, lambda v, j: over_slot(v, 1))
    sum_a = step(sum_a, 0, lambda v, j: over_slot(v, 2 * j))
    sum_b = step(sum_b, 0, lambda v, j: over_query(v, 1))
    sum_a = step(sum_a, 0, lambda v, j: over_query(v, 1))
    sum_b = step(sum_b, 0, lambda v, j: over_slot(v, 2 * j))
    both = jnp.concatenate([sum_a, sum_b], axis=1)
    own_block = step(both, 0, lambda v, j: over_query(v, 2 * j))

    pay_near, pay_far = gather_query(pay)
    feed, info = feed_grads(
        micro,
        masked,
        x_split,
        ids,
        pay_near,
        pay_far,
        first_near,
        first_far,
        active_q,
        slope_q,
        w_ffn_out,
    )
    feed = step(feed.reshape((2, x_split) + feed.shape[1:]), 0, lambda v, j: over_slot(v, 1))
    feed = step(feed, 0, lambda v, j: over_slot(v, 2 * j))

    piece = jnp.concatenate([own_block, feed], axis=0)
    if x_split < n_x:
        terms = [over_slot(piece.astype(BF), 2 * j).astype(F32) for j in range(1, n_x)]
        piece = functools.reduce(jnp.add, terms, piece)
    piece = piece.astype(BF)
    pieces = jnp.stack([piece] + [over_slot(piece, 2 * j) for j in range(1, x_split)])
    other = over_slot(pieces, 1)
    w_out_grad, w_qkv_grad, w_in_grad, w_ffn_grad, w_retr_grad, vec = assemble(
        n_q, x_split, inner, rd, ids, pieces, other
    )
    half = width // 2
    b_in_grad = lax.dynamic_slice_in_dim(
        vec[:8].reshape(-1), q_me * (inner // n_q), inner // n_q, 0
    )
    vec = jnp.concatenate([vec[8:16], vec[16:]], axis=1)
    vec = lax.dynamic_slice_in_dim(vec, q_me * (width // n_q), width // n_q, 1)

    picked_q = jnp.concatenate([near, far], axis=0).reshape(n_q * own_rows, width)
    picked_all = lax.all_gather(picked_q, "slot", axis=0, tiled=True)
    row_info = jnp.concatenate(
        [
            info.reshape(n_q * own_rows, 128)[:, :2].T,
            jnp.take(local_targets, q_order, axis=0).reshape(1, -1).astype(F32),
        ],
        axis=0,
    )
    all_info = lax.all_gather(row_info, "slot", axis=0).transpose(1, 0, 2).reshape(3, -1)
    all_targets = all_info[2:].astype(jnp.int32)
    tile = next(t for t in (256, 192, 128) if vocab_own % t == 0)
    n_tiles = vocab_own // tile
    table_grad = None
    first_tile = 0
    while first_tile < n_tiles:
        count = min(5, n_tiles - first_tile)
        table_grad = table_grad_part(
            first_tile, count, tile, all_info, all_targets, picked_all, word_table, table_grad
        )
        first_tile += count

    back_rows = times_transposed(query_low, w_qkv[:, :width]) + scaled_one
    row_ok = lax.iota(jnp.int32, n_rows) < own_rows + micro
    place = (token_of == lax.iota(jnp.int32, tokens)[None, :]) & row_ok[:, None]
    hidden_grad = times_transposed(kv_grad, w_qkv[:, width:]) + lax.dot_general(
        place.astype(F32),
        back_rows,
        (((0,), (0,)), ((), ())),
        precision=TOP_PRECISION,
        preferred_element_type=F32,
    )

    return (
        marginal,
        layer_out.reshape(hidden_in.shape),
        hidden_grad.reshape(hidden_in.shape),
        query_grad,
        w_qkv_grad,
        vec[0],
        vec[1],
        w_out_grad,
        vec[2],
        vec[3],
        vec[4],
        w_in_grad,
        b_in_grad,
        w_ffn_grad,
        vec[7],
        vec[5],
        vec[6],
        w_retr_grad,
        table_grad,
    )


def solution(mesh):
    return jax.shard_map(
        functools.partial(per_device, mesh.shape["query"], mesh.shape["slot"]),
        mesh=mesh,
        in_specs=(
            P(None, "query", "slot", None, None),
            P(None, "query", "slot", None),
            P(None, "query", "slot", None),
            P(None, None, "slot", None),
            P(None, "query", "slot"),
            P(None, "query", "slot"),
            P(),
            P(),
            P(),
            P(),
            P(),
            P(),
            P(),
            P(),
            P(),
            P(),
            P(),
            P(),
            P(),
            P(),
            P("query", None),
        ),
        out_specs=(
            P(None, "query"),
            P(None, "query", "slot", None, None),
            P(None, "query", "slot", None, None),
            P(None, "query", "slot"),
            P("query", None),
            P("query"),
            P("query"),
            P("query", None),
            P("query"),
            P("query"),
            P("query"),
            P("query", None),
            P("query"),
            P("query", None),
            P("query"),
            P("query"),
            P("query"),
            P("query", None),
            P("query", None),
        ),
        check_vma=False,
    )
```
